512 devices in a mesh: dom: 128 (over z, y, core), rep: 4 (over x).
Axes of the slice: x: 4, y: 8, z: 8, core: 2. Of those that a mesh axis runs over, the one named last changes fastest.
Arguments:
- embedding: bfloat16 [131072, 128], P('dom'), may hold values from -6 to 6
- cotangent: bfloat16 [131072, 128], P('dom'), may hold values from -6 to 6
- degrees: int32 [131072], P('dom'), may hold values from 2 to 64
- tile_values: bfloat16 [128, 4, 32, 128, 128], P('dom', 'rep'), may hold values from 0 to 2, as said below
- tile_target: int32 [128, 4, 32], P('dom', 'rep'), may hold values from 0 to 7
- tile_source: int32 [128, 4, 32], P('dom', 'rep'), may hold values from 0 to 27
- live_tile_count: int32 [128, 4], P('dom', 'rep'), may hold values from 4 to 32, as said below
- send_rows: int32 [128, 128, 16], P('dom'), may hold values from 0 to 1023
- hub_rows: int32 [128, 4], P('dom'), may hold values from 0 to 1023
Outputs:
- layer_output: bfloat16 [131072, 128], P(('dom', 'rep'))
- embedding_gradient: bfloat16 [131072, 128], P(('dom', 'rep'))
The draws below stay inside these ranges and needn't reach their ends.
Inputs may be any that keep to these rules, and one draw needn't show every extreme that they name: `tile_values`: each entry is an edge weight, zero where the two nodes share no edge. `live_tile_count`: slots at or past a device's count are not live; in every draw some device has all 32 slots live.
All inputs are finite; a program needn't handle non-finite values.
Results may differ from the reference program's by a relative error of at most 0.0048.
Values may be sent and summed in bfloat16 or wider, within the bound.
No kernel may reach another device: no remote copies, remote signals or barrier semaphores. Data moves between devices by JAX's collectives and lax.ppermute only.
A program may use at most 64 MiB of HBM per device.

```python
import jax
import jax.numpy as jnp
from jax import lax

D = 128
TB = 128
ROWS_PART = 1024
TILES_DEV = 32
BOUND = 2048
HUBS = 512
BPAIR = 16
HUB_DEV = 4
NODES = 131072
N_DOM = 128
N_REP = 4


def draw_tile_values(key, part):
    shape = (N_DOM, N_REP, TILES_DEV, TB, TB)
    uniform_draw = jax.random.uniform(jax.random.fold_in(key, 11), shape, jnp.float32)
    values = jnp.where(uniform_draw < 0.25, 0.5 * jnp.exp(5.545177 * uniform_draw), 0.0)
    return values.astype(jnp.float32).astype(jnp.bfloat16)


def draw_live_tile_count(key, part):
    first_key, second_key = jax.random.split(jax.random.fold_in(key, 7))
    device_total = N_DOM * N_REP
    exponent = jax.random.randint(first_key, (device_total,), 1, 4)
    counts = jnp.right_shift(jnp.full((device_total,), TILES_DEV, jnp.int32), exponent.astype(jnp.int32))
    selected_tiles = jax.random.randint(second_key, (), 0, device_total)
    counts = jnp.where(jnp.arange(device_total) == selected_tiles, TILES_DEV, counts)
    return counts.reshape(N_DOM, N_REP).astype(jnp.int32)


def touch_ends(entries, own_key, smallest, largest):
    index_at = [jax.random.randint(jax.random.fold_in(own_key, axis), (), 0, length) for axis, length in enumerate(entries.shape)]
    longest = entries.shape.index(max(entries.shape))
    beside = index_at[:longest] + [(index_at[longest] + 1) % entries.shape[longest]] + index_at[longest + 1:]
    return entries.at[tuple(index_at)].set(smallest).at[tuple(beside)].set(largest)


def block_levels(rng, dims, pieces, low, high):
    level = 1.0
    for dim, shards_of in pieces:
        steps = jax.random.uniform(jax.random.fold_in(jax.random.fold_in(rng, 6), dim), (shards_of,), jnp.float32, low / len(pieces), high / len(pieces))
        level = level * jnp.repeat(jnp.exp(steps), dims[dim] // shards_of).reshape((-1,) + (1,) * (len(dims) - 1 - dim))
    return level


def gaussian(stream_key, shape, width, limit, shards=(), held_as=jnp.bfloat16):
    array = jax.random.normal(stream_key, shape, jnp.float32) * width
    if len(shards) > 0:
        array = block_levels(stream_key, shape, shards, -0.22, 0.18) * array
    return jnp.clip(array, min=-limit, max=limit).astype(held_as)


def setup_inputs(seed: int = 0) -> dict:
    seeds = jax.random.split(jax.random.key(seed), 10)
    return {
        "embedding": gaussian(seeds[0], (NODES, D), 1.0, 6.0, ((0, 128),)),
        "cotangent": gaussian(seeds[1], (NODES, D), 1.0, 6.0, ((0, 128),)),
        "degrees": touch_ends(jax.random.randint(seeds[2], (NODES,), 2, 65), jax.random.fold_in(seeds[2], 1), 2, 64).astype(jnp.int32),
        "tile_values": draw_tile_values(jax.random.fold_in(seeds[9], 71), 0),
        "tile_target": touch_ends(jax.random.randint(seeds[4], (N_DOM, N_REP, TILES_DEV), 0, ROWS_PART // TB), jax.random.fold_in(seeds[4], 1), 0, (ROWS_PART // TB) - 1).astype(jnp.int32),
        "tile_source": touch_ends(jax.random.randint(seeds[5], (N_DOM, N_REP, TILES_DEV), 0, (ROWS_PART + BOUND + HUBS) // TB), jax.random.fold_in(seeds[5], 1), 0, ((ROWS_PART + BOUND + HUBS) // TB) - 1).astype(jnp.int32),
        "live_tile_count": draw_live_tile_count(jax.random.fold_in(seeds[9], 71), 0),
        "send_rows": touch_ends(jax.random.randint(seeds[7], (N_DOM, N_DOM, BPAIR), 0, ROWS_PART), jax.random.fold_in(seeds[7], 1), 0, ROWS_PART - 1).astype(jnp.int32),
        "hub_rows": touch_ends(jax.random.randint(seeds[8], (N_DOM, HUB_DEV), 0, ROWS_PART), jax.random.fold_in(seeds[8], 1), 0, ROWS_PART - 1).astype(jnp.int32),
    }


def reference(embedding, cotangent, degrees, tile_values, tile_target, tile_source, live_tile_count, send_rows, hub_rows):
    feature_width = embedding.shape[1]
    root_inverse = lax.rsqrt(degrees.astype(jnp.float32))
    scaled = (root_inverse[:, None] * embedding.astype(jnp.float32)).astype(jnp.bfloat16)
    weighted = (root_inverse[:, None] * cotangent.astype(jnp.float32)).astype(jnp.bfloat16)
    owned_rows = scaled.reshape(N_DOM, ROWS_PART, feature_width)
    owned_weighted = weighted.reshape(N_DOM, ROWS_PART, feature_width)
    owners = jnp.arange(N_DOM, dtype=jnp.int32)[:, None]
    hub_block = owned_rows[owners, hub_rows].reshape(HUBS, feature_width)
    target_blocks = ROWS_PART // TB
    source_total = ROWS_PART + BOUND + HUBS
    source_blocks = source_total // TB
    slot_indices = jnp.arange(TILES_DEV, dtype=jnp.int32)

    def one_partition(totals, device_portion):
        boundary = owned_rows[owners, send_rows[:, device_portion, :]].reshape(BOUND, feature_width)
        source = jnp.concatenate([owned_rows[device_portion], boundary, hub_block], 0)
        source = source.reshape(source_blocks, TB, feature_width)
        target = owned_weighted[device_portion].reshape(target_blocks, TB, feature_width)
        forward = jnp.zeros((target_blocks, TB, feature_width), jnp.float32)
        backward = jnp.zeros((source_blocks, TB, feature_width), jnp.float32)
        for replica_index in range(N_REP):
            tile_matrix_block = tile_values[device_portion, replica_index].astype(jnp.float32)
            tile_alive_mask = (slot_indices < live_tile_count[device_portion, replica_index]).astype(jnp.float32)[:, None, None]
            targets = tile_target[device_portion, replica_index]
            sources = tile_source[device_portion, replica_index]
            selected_entries = source[sources].astype(jnp.float32)
            message_product = jnp.einsum('ack,aky->acy', tile_matrix_block, selected_entries, precision=lax.Precision.HIGHEST) * tile_alive_mask
            forward = forward + jax.ops.segment_sum(message_product, targets, num_segments=target_blocks)
            selected_tiles = target[targets].astype(jnp.float32)
            gathered_portion = jnp.einsum('vzr,vzu->vru', tile_matrix_block, selected_tiles, precision=lax.Precision.HIGHEST) * tile_alive_mask
            backward = backward + jax.ops.segment_sum(gathered_portion, sources, num_segments=source_blocks)
        backward = backward.reshape(source_total, feature_width)
        totals = totals.at[device_portion].add(backward[:ROWS_PART])
        boundary_part = backward[ROWS_PART:ROWS_PART + BOUND].reshape(N_DOM, BPAIR, feature_width)
        totals = totals.at[owners, send_rows[:, device_portion, :]].add(boundary_part)
        hub_part = backward[ROWS_PART + BOUND:].reshape(N_DOM, HUB_DEV, feature_width)
        totals = totals.at[owners, hub_rows].add(hub_part)
        return (totals, forward.reshape(ROWS_PART, feature_width))
    start = jnp.zeros((N_DOM, ROWS_PART, feature_width), jnp.float32)
    totals, forward_sum = lax.scan(one_partition, start, jnp.arange(N_DOM, dtype=jnp.int32))
    layer_output = (root_inverse[:, None] * forward_sum.reshape(NODES, feature_width)).astype(jnp.bfloat16)
    embedding_gradient = (root_inverse[:, None] * totals.reshape(NODES, feature_width)).astype(jnp.bfloat16)
    return (layer_output, embedding_gradient)
```

```python
import jax
import jax.numpy as jnp
from jax import lax
from jax.experimental import pallas as pl
from jax.experimental.pallas import tpu as pltpu
from jax.sharding import PartitionSpec as P

TB = 128
GROUP = 4


def _column(row):
    return jnp.broadcast_to(row, (TB, TB)).T


def _tile_loop(live, step):
    def group(g, carry):
        step(g * GROUP)
        return carry

    lax.fori_loop(0, (live + GROUP - 1) // GROUP, group, 0)


def _before_kernel(live_ref, target_ref, source_ref, hub_ref, degrees_ref, rows_ref, embedding_ref,
                   cotangent_ref, tiles_ref, send_ref, local_ref, scaled_ref, weighted_ref, slots_ref):
    f32, bf16 = jnp.float32, jnp.bfloat16
    own_blocks = degrees_ref.shape[0]
    half = own_blocks // 2
    bound_blocks = rows_ref.shape[0]
    root = lax.rsqrt(degrees_ref[...].astype(f32))
    for b in range(own_blocks):
        part = slice(b * TB, (b + 1) * TB)
        column = _column(root[b:b + 1])
        scaled_ref[part] = (column * embedding_ref[part].astype(f32)).astype(bf16)
        weighted_ref[part] = (column * cotangent_ref[part].astype(f32)).astype(bf16)

    halves = jnp.concatenate([scaled_ref[:half * TB], scaled_ref[half * TB:]], axis=1)
    lane = lax.broadcasted_iota(jnp.int32, (TB, TB), 1)

    def pick(index, count):
        high = index >= half * TB
        low = jnp.where(high, index - half * TB, index)
        onehot = jnp.concatenate(
            [(low == lane[:count] + j * TB).astype(f32).astype(bf16) for j in range(half)], axis=1)
        both = jnp.dot(onehot, halves, preferred_element_type=f32)
        return jnp.where(high, both[:, TB:], both[:, :TB])

    for i in range(bound_blocks):
        index = _column(rows_ref[i:i + 1].astype(f32)).astype(jnp.int32)
        send_ref[8 * i:8 * i + 8, 0:16, :] = pick(index, TB).astype(bf16).reshape(8, 16, TB)
    sub = lax.broadcasted_iota(jnp.int32, (16, TB), 0)
    index = jnp.zeros((16, TB), jnp.int32)
    for j in range(4):
        index = jnp.where(sub == j, hub_ref[j], index)
    hub = pick(index, 16)[:8]

    slots_ref[...] = jnp.zeros(slots_ref.shape, f32)
    live = live_ref[0]

    def step(t):
        products = []
        for k in range(GROUP):
            target = target_ref[t + k]
            w = weighted_ref[pl.ds(pl.multiple_of(target * TB, TB), TB), :]
            products.append(lax.dot_general(
                tiles_ref[t + k], w, (((0,), (0,)), ((), ())), preferred_element_type=f32))
        for k in range(GROUP):
            slots_ref[source_ref[t + k]] += jnp.where(t + k < live, products[k], 0.0)

    _tile_loop(live, step)
    local_ref[...] = slots_ref[:own_blocks].reshape(own_blocks * TB, TB)
    for i in range(bound_blocks):
        send_ref[8 * i:8 * i + 8, 16:32, :] = slots_ref[own_blocks + i].astype(bf16).reshape(8, 16, TB)
    first = lax.broadcasted_iota(jnp.int32, (16, 8, TB), 1) < 4
    hub_tile = jnp.broadcast_to(hub[None], (16, 8, TB))
    for h in range(slots_ref.shape[0] - own_blocks - bound_blocks):
        x = slots_ref[own_blocks + bound_blocks + h].reshape(16, 8, TB)
        odd = jnp.where(first, hub_tile, x)
        even = jnp.where(first, hub_tile, pltpu.roll(x, 4, 1))
        pair = jnp.stack([even, odd], axis=1).reshape(32, 8, TB)
        send_ref[32 * h:32 * h + 32, 32:40, :] = pair.astype(bf16)


def _after_kernel(live_ref, target_ref, source_ref, hub_ref, degrees_ref, rows_ref, arrived_ref, local_ref,
                  scaled_ref, tiles_ref, out_ref, source_rows_ref, forward_ref, gradient_ref):
    f32, bf16 = jnp.float32, jnp.bfloat16
    own_blocks = degrees_ref.shape[0]
    bound_blocks = rows_ref.shape[0]
    for b in range(own_blocks):
        source_rows_ref[b] = scaled_ref[b * TB:(b + 1) * TB]
    for i in range(bound_blocks):
        source_rows_ref[own_blocks + i] = arrived_ref[8 * i:8 * i + 8, 0:16, :].reshape(TB, TB)
    first = lax.broadcasted_iota(jnp.int32, (16, 8, TB), 1) < 4
    hub_total = jnp.zeros((8, TB), f32)
    for h in range(source_rows_ref.shape[0] - own_blocks - bound_blocks):
        x = arrived_ref[32 * h:32 * h + 32, 32:40, :].astype(f32)
        hub_total = hub_total + jnp.sum(x, axis=0)
        x = x.reshape(16, 2, 8, TB)
        merged = jnp.where(first, x[:, 0], pltpu.roll(x[:, 1], 4, 1))
        source_rows_ref[own_blocks + bound_blocks + h] = merged.reshape(TB, TB).astype(bf16)

    forward_ref[...] = jnp.zeros(forward_ref.shape, f32)
    live = live_ref[0]

    def step(t):
        products = [
            jnp.dot(tiles_ref[t + k], source_rows_ref[source_ref[t + k]], preferred_element_type=f32)
            for k in range(GROUP)
        ]
        for k in range(GROUP):
            forward_ref[target_ref[t + k]] += jnp.where(t + k < live, products[k], 0.0)

    _tile_loop(live, step)

    returned = arrived_ref[:, 16:32, :].reshape(bound_blocks * TB, TB)
    sub = lax.broadcasted_iota(jnp.int32, (TB, TB), 0)
    for b in range(own_blocks):
        onehot = jnp.concatenate(
            [(jnp.broadcast_to(rows_ref[i:i + 1], (TB, TB)) == sub + b * TB).astype(f32).astype(bf16)
             for i in range(bound_blocks)], axis=1)
        part = slice(b * TB, (b + 1) * TB)
        gradient_ref[part] = local_ref[part] + jnp.dot(onehot, returned, preferred_element_type=f32)
    for j in range(4):
        row = pl.ds(hub_ref[j], 1)
        gradient_ref[row, :] = gradient_ref[row, :] + hub_total[4 + j:5 + j]

    root = lax.rsqrt(degrees_ref[...].astype(f32))
    replicas = out_ref.shape[0]
    each = own_blocks // replicas
    for b in range(own_blocks):
        column = _column(root[b:b + 1])
        c, at = b // each, (b % each) * TB
        out_ref[c, at:at + TB] = (column * forward_ref[b]).astype(bf16)
        at += each * TB
        out_ref[c, at:at + TB] = (column * gradient_ref[b * TB:(b + 1) * TB]).astype(bf16)


def body(embedding, cotangent, degrees, tile_values, tile_target, tile_source, live_tile_count, send_rows, hub_rows):
    f32, bf16 = jnp.float32, jnp.bfloat16
    own_rows, width = embedding.shape
    slots = tile_values.shape[2]
    partitions, pair_rows = send_rows.shape[1:]
    hubs = hub_rows.shape[1]
    replicas = lax.axis_size("rep")
    own_blocks = own_rows // TB
    source_blocks = (own_rows + partitions * (pair_rows + hubs)) // TB
    tiles = tile_values.reshape(slots, TB, TB)
    small = (live_tile_count.reshape(1), tile_target.reshape(slots), tile_source.reshape(slots), hub_rows.reshape(hubs))
    degree_blocks = degrees.reshape(own_blocks, TB)
    rows = send_rows.reshape(partitions * pair_rows // TB, TB)
    in_smem = pl.BlockSpec(memory_space=pltpu.SMEM)
    in_vmem = pl.BlockSpec(memory_space=pltpu.VMEM)
    pair = 2 * (pair_rows + hubs)

    send, local, scaled = pl.pallas_call(
        _before_kernel,
        out_shape=(
            jax.ShapeDtypeStruct((partitions, pair, width), bf16),
            jax.ShapeDtypeStruct((own_rows, width), f32),
            jax.ShapeDtypeStruct((own_rows, width), bf16),
        ),
        in_specs=[in_smem] * 4 + [in_vmem] * 5,
        out_specs=(in_vmem,) * 3,
        scratch_shapes=[pltpu.VMEM((own_rows, width), bf16), pltpu.VMEM((source_blocks, TB, width), f32)],
        name="before",
    )(*small, degree_blocks, rows, embedding, cotangent, tiles)

    arrived = lax.all_to_all(send, "dom", split_axis=0, concat_axis=0, tiled=True)

    exchange = pl.pallas_call(
        _after_kernel,
        out_shape=jax.ShapeDtypeStruct((replicas, 2 * own_rows // replicas, width), bf16),
        in_specs=[in_smem] * 4 + [in_vmem] * 6,
        out_specs=in_vmem,
        scratch_shapes=[
            pltpu.VMEM((source_blocks, TB, width), bf16),
            pltpu.VMEM((own_blocks, TB, width), f32),
            pltpu.VMEM((own_rows, width), f32),
        ],
        name="after",
    )(*small, degree_blocks, rows, arrived, local, scaled, tiles)

    parts = lax.all_to_all(exchange, "rep", split_axis=0, concat_axis=0, tiled=True)
    total = jnp.sum(parts.astype(f32), axis=0).astype(bf16)
    out_rows = own_rows // replicas
    return total[:out_rows], total[out_rows:]


def solution(mesh):
    placed = (
        P("dom", None),
        P("dom", None),
        P("dom"),
        P("dom", "rep", None, None, None),
        P("dom", "rep", None),
        P("dom", "rep", None),
        P("dom", "rep"),
        P("dom", None, None),
        P("dom", None),
    )
    return jax.shard_map(
        body,
        mesh=mesh,
        in_specs=placed,
        out_specs=(P(("dom", "rep"), None), P(("dom", "rep"), None)),
        check_vma=False,
    )
```

```python
import jax
import jax.numpy as jnp
from jax import lax
from jax.experimental import pallas as pl
from jax.experimental.pallas import tpu as pltpu
from jax.sharding import PartitionSpec as P

TB = 128
GROUP = 4


def _column(row):
    return jnp.broadcast_to(row, (TB, TB)).T


def _tile_loop(live, step):
    def group(g, carry):
        step(g * GROUP)
        return carry

    lax.fori_loop(0, (live + GROUP - 1) // GROUP, group, 0)


def _gather_kernel(hub_ref, degrees_ref, rows_ref, embedding_ref, send_ref, scaled_ref, hub_rows_ref, order_ref):
    f32, bf16 = jnp.float32, jnp.bfloat16
    own_blocks = degrees_ref.shape[0]
    half = own_blocks // 2
    pair_rows = rows_ref.shape[0]
    root = lax.rsqrt(degrees_ref[...].astype(f32))
    for b in range(own_blocks):
        part = slice(b * TB, (b + 1) * TB)
        scaled_ref[part] = (_column(root[b:b + 1]) * embedding_ref[part].astype(f32)).astype(bf16)

    halves = jnp.concatenate([scaled_ref[:half * TB], scaled_ref[half * TB:]], axis=1)
    lane = lax.broadcasted_iota(jnp.int32, (TB, TB), 1)

    def pick(index, count):
        high = index >= half * TB
        low = jnp.where(high, index - half * TB, index)
        onehot = jnp.concatenate(
            [(low == lane[:count] + j * TB).astype(f32).astype(bf16) for j in range(half)], axis=1)
        both = jnp.dot(onehot, halves, preferred_element_type=f32)
        return jnp.where(high, both[:, TB:], both[:, :TB])

    for k in range(pair_rows):
        index = _column(rows_ref[k:k + 1].astype(f32)).astype(jnp.int32)
        order_ref[pl.ds(k, TB, stride=pair_rows), :] = pick(index, TB)
    send_ref[...] = order_ref[...].astype(bf16).reshape(send_ref.shape)
    sub = lax.broadcasted_iota(jnp.int32, (16, TB), 0)
    index = jnp.zeros((16, TB), jnp.int32)
    for j in range(4):
        index = jnp.where(sub == j, hub_ref[j], index)
    hub_rows_ref[...] = pick(index, 16)[:8]


def _backward_kernel(live_ref, target_ref, source_ref, degrees_ref, cotangent_ref, hub_rows_ref, tiles_ref,
                     send_ref, local_ref, weighted_ref, slots_ref):
    f32, bf16 = jnp.float32, jnp.bfloat16
    own_blocks = degrees_ref.shape[0]
    bound_blocks = send_ref.shape[0] // 8
    root = lax.rsqrt(degrees_ref[...].astype(f32))
    for b in range(own_blocks):
        part = slice(b * TB, (b + 1) * TB)
        weighted_ref[part] = (_column(root[b:b + 1]) * cotangent_ref[part].astype(f32)).astype(bf16)
    slots_ref[...] = jnp.zeros(slots_ref.shape, f32)
    live = live_ref[0]

    def step(t):
        products = []
        for k in range(GROUP):
            target = target_ref[t + k]
            w = weighted_ref[pl.ds(pl.multiple_of(target * TB, TB), TB), :]
            products.append(lax.dot_general(
                tiles_ref[t + k], w, (((0,), (0,)), ((), ())), preferred_element_type=f32))
        for k in range(GROUP):
            slots_ref[source_ref[t + k]] += jnp.where(t + k < live, products[k], 0.0)

    _tile_loop(live, step)
    local_ref[...] = slots_ref[:own_blocks].reshape(own_blocks * TB, TB)
    for i in range(bound_blocks):
        send_ref[8 * i:8 * i + 8, 0:16, :] = slots_ref[own_blocks + i].astype(bf16).reshape(8, 16, TB)
    first = lax.broadcasted_iota(jnp.int32, (16, 8, TB), 1) < 4
    hub_tile = jnp.broadcast_to(hub_rows_ref[...][None], (16, 8, TB))
    for h in range(slots_ref.shape[0] - own_blocks - bound_blocks):
        x = slots_ref[own_blocks + bound_blocks + h].reshape(16, 8, TB)
        odd = jnp.where(first, hub_tile, x)
        even = jnp.where(first, hub_tile, pltpu.roll(x, 4, 1))
        pair = jnp.stack([even, odd], axis=1).reshape(32, 8, TB)
        send_ref[32 * h:32 * h + 32, 16:24, :] = pair.astype(bf16)


def _forward_kernel(live_ref, target_ref, source_ref, arrived_ref, scaled_ref, tiles_ref, forward_ref, source_rows_ref):
    f32 = jnp.float32
    own_blocks = forward_ref.shape[0]
    bound_blocks = arrived_ref.shape[0] // 8
    for b in range(own_blocks):
        source_rows_ref[b] = scaled_ref[b * TB:(b + 1) * TB]
    for i in range(bound_blocks):
        source_rows_ref[own_blocks + i] = arrived_ref[8 * i:8 * i + 8].reshape(TB, TB)
    forward_ref[...] = jnp.zeros(forward_ref.shape, f32)
    live = live_ref[0]
    here = own_blocks + bound_blocks

    def step(t):
        products = [
            jnp.dot(tiles_ref[t + k], source_rows_ref[jnp.minimum(source_ref[t + k], here - 1)],
                    preferred_element_type=f32) for k in range(GROUP)
        ]
        for k in range(GROUP):
            use = jnp.logical_and(t + k < live, source_ref[t + k] < here)
            forward_ref[target_ref[t + k]] += jnp.where(use, products[k], 0.0)

    _tile_loop(live, step)


def _finish_kernel(live_ref, target_ref, source_ref, hub_ref, degrees_ref, rows_ref, arrived_ref, local_ref,
                   early_ref, tiles_ref, out_ref, source_rows_ref, forward_ref, gradient_ref):
    f32, bf16 = jnp.float32, jnp.bfloat16
    own_blocks = degrees_ref.shape[0]
    bound_blocks = rows_ref.shape[0]
    first = lax.broadcasted_iota(jnp.int32, (16, 8, TB), 1) < 4
    hub_total = jnp.zeros((8, TB), f32)
    for h in range(source_rows_ref.shape[0]):
        x = arrived_ref[32 * h:32 * h + 32, 16:24, :].astype(f32)
        hub_total = hub_total + jnp.sum(x, axis=0)
        x = x.reshape(16, 2, 8, TB)
        merged = jnp.where(first, x[:, 0], pltpu.roll(x[:, 1], 4, 1))
        source_rows_ref[h] = merged.reshape(TB, TB).astype(bf16)
    forward_ref[...] = early_ref[...]
    here = own_blocks + bound_blocks

    def slot(t, carry):
        @pl.when(source_ref[t] >= here)
        def _():
            forward_ref[target_ref[t]] += jnp.dot(
                tiles_ref[t], source_rows_ref[source_ref[t] - here], preferred_element_type=f32)
        return carry

    lax.fori_loop(0, live_ref[0], slot, 0)

    returned = arrived_ref[:, 0:16, :].reshape(bound_blocks * TB, TB)
    sub = lax.broadcasted_iota(jnp.int32, (TB, TB), 0)
    for b in range(own_blocks):
        onehot = jnp.concatenate(
            [(jnp.broadcast_to(rows_ref[i:i + 1], (TB, TB)) == sub + b * TB).astype(f32).astype(bf16)
             for i in range(bound_blocks)], axis=1)
        part = slice(b * TB, (b + 1) * TB)
        gradient_ref[part] = local_ref[part] + jnp.dot(onehot, returned, preferred_element_type=f32)
    for j in range(4):
        row = pl.ds(hub_ref[j], 1)
        gradient_ref[row, :] = gradient_ref[row, :] + hub_total[4 + j:5 + j]

    root = lax.rsqrt(degrees_ref[...].astype(f32))
    each = own_blocks // out_ref.shape[0]
    for b in range(own_blocks):
        column = _column(root[b:b + 1])
        c, at = b // each, (b % each) * TB
        out_ref[c, at:at + TB] = (column * forward_ref[b]).astype(bf16)
        at += each * TB
        out_ref[c, at:at + TB] = (column * gradient_ref[b * TB:(b + 1) * TB]).astype(bf16)


def body(embedding, cotangent, degrees, tile_values, tile_target, tile_source, live_tile_count, send_rows, hub_rows):
    f32, bf16 = jnp.float32, jnp.bfloat16
    own_rows, width = embedding.shape
    slots = tile_values.shape[2]
    partitions, pair_rows = send_rows.shape[1:]
    hubs = hub_rows.shape[1]
    replicas = lax.axis_size("rep")
    own_blocks = own_rows // TB
    source_blocks = (own_rows + partitions * (pair_rows + hubs)) // TB
    tiles = tile_values.reshape(slots, TB, TB)
    live, target, source, hub = (
        live_tile_count.reshape(1), tile_target.reshape(slots), tile_source.reshape(slots), hub_rows.reshape(hubs))
    degree_blocks = degrees.reshape(own_blocks, TB)
    rows = send_rows.reshape(partitions * pair_rows // TB, TB)
    rows_by_place = send_rows[0].T
    in_smem = pl.BlockSpec(memory_space=pltpu.SMEM)
    in_vmem = pl.BlockSpec(memory_space=pltpu.VMEM)
    shape = jax.ShapeDtypeStruct

    forward_rows, scaled, hub_own = pl.pallas_call(
        _gather_kernel,
        out_shape=(shape((partitions, pair_rows, width), bf16), shape((own_rows, width), bf16), shape((8, width), f32)),
        in_specs=[in_smem] + [in_vmem] * 3,
        out_specs=(in_vmem,) * 3,
        scratch_shapes=[pltpu.VMEM((partitions * pair_rows, width), f32)],
        name="gather",
    )(hub, degree_blocks, rows_by_place, embedding)
    arrived = lax.all_to_all(forward_rows, "dom", split_axis=0, concat_axis=0, tiled=True)

    partials, local = pl.pallas_call(
        _backward_kernel,
        out_shape=(shape((partitions, pair_rows + 2 * hubs, width), bf16), shape((own_rows, width), f32)),
        in_specs=[in_smem] * 3 + [in_vmem] * 4,
        out_specs=(in_vmem,) * 2,
        scratch_shapes=[pltpu.VMEM((own_rows, width), bf16), pltpu.VMEM((source_blocks, TB, width), f32)],
        name="backward",
    )(live, target, source, degree_blocks, cotangent, hub_own, tiles)
    returned = lax.all_to_all(partials, "dom", split_axis=0, concat_axis=0, tiled=True)

    early = pl.pallas_call(
        _forward_kernel,
        out_shape=shape((own_blocks, TB, width), f32),
        in_specs=[in_smem] * 3 + [in_vmem] * 3,
        out_specs=in_vmem,
        scratch_shapes=[pltpu.VMEM((own_blocks + partitions * pair_rows // TB, TB, width), bf16)],
        name="forward",
    )(live, target, source, arrived, scaled, tiles)

    exchange = pl.pallas_call(
        _finish_kernel,
        out_shape=shape((replicas, 2 * own_rows // replicas, width), bf16),
        in_specs=[in_smem] * 4 + [in_vmem] * 6,
        out_specs=in_vmem,
        scratch_shapes=[
            pltpu.VMEM((partitions * hubs // TB, TB, width), bf16),
            pltpu.VMEM((own_blocks, TB, width), f32),
            pltpu.VMEM((own_rows, width), f32),
        ],
        name="finish",
    )(live, target, source, hub, degree_blocks, rows, returned, local, early, tiles)

    parts = lax.all_to_all(exchange, "rep", split_axis=0, concat_axis=0, tiled=True)
    total = jnp.sum(parts.astype(f32), axis=0).astype(bf16)
    out_rows = own_rows // replicas
    return total[:out_rows], total[out_rows:]


def solution(mesh):
    placed = (
        P("dom", None),
        P("dom", None),
        P("dom"),
        P("dom", "rep", None, None, None),
        P("dom", "rep", None),
        P("dom", "rep", None),
        P("dom", "rep"),
        P("dom", None, None),
        P("dom", None),
    )
    return jax.shard_map(
        body,
        mesh=mesh,
        in_specs=placed,
        out_specs=(P(("dom", "rep"), None), P(("dom", "rep"), None)),
        check_vma=False,
    )
```

```python
import jax
import jax.numpy as jnp
from jax import lax
from jax.experimental import pallas as pl
from jax.experimental.pallas import tpu as pltpu
from jax.sharding import PartitionSpec as P

TB = 128
GROUP = 4


def _column(row):
    return jnp.broadcast_to(row, (TB, TB)).T


def _tile_loop(live, step):
    def group(g, carry):
        step(g * GROUP)
        return carry

    lax.fori_loop(0, (live + GROUP - 1) // GROUP, group, 0)


def _fetch(pairs, sems):
    copies = [pltpu.make_async_copy(src, dst, sems.at[i]) for i, (src, dst) in enumerate(pairs)]
    for copy in copies:
        copy.start()
    return copies


def _before_kernel(live_hbm, target_hbm, source_hbm, hub_hbm, degrees_hbm, rows_hbm, embedding_hbm, cotangent_hbm,
                   tiles_hbm, send_hbm, local_hbm, scaled_hbm, live_ref, target_ref, source_ref, hub_ref, degrees_ref,
                   rows_ref, embedding_ref, cotangent_ref, tiles_ref, early_ref, late_ref, scaled_ref, weighted_ref,
                   slots_ref, order_ref, sems):
    f32, bf16 = jnp.float32, jnp.bfloat16
    copies = _fetch((
        (degrees_hbm, degrees_ref), (embedding_hbm, embedding_ref), (rows_hbm, rows_ref), (hub_hbm, hub_ref),
        (cotangent_hbm, cotangent_ref), (live_hbm, live_ref), (target_hbm, target_ref), (source_hbm, source_ref),
        (tiles_hbm, tiles_ref)), sems)
    own_blocks = degrees_ref.shape[0]
    half = own_blocks // 2
    pair_rows = rows_ref.shape[0]
    bound_blocks = send_hbm.shape[0] // 8
    slots_ref[...] = jnp.zeros(slots_ref.shape, f32)
    for copy in copies[:4]:
        copy.wait()
    root = lax.rsqrt(degrees_ref[...].astype(f32))
    for b in range(own_blocks):
        part = slice(b * TB, (b + 1) * TB)
        scaled_ref[part] = (_column(root[b:b + 1]) * embedding_ref[part].astype(f32)).astype(bf16)

    halves = jnp.concatenate([scaled_ref[:half * TB], scaled_ref[half * TB:]], axis=1)
    lane = lax.broadcasted_iota(jnp.int32, (TB, TB), 1)

    def pick(index, count):
        high = index >= half * TB
        low = jnp.where(high, index - half * TB, index)
        onehot = jnp.concatenate(
            [(low == lane[:count] + j * TB).astype(f32).astype(bf16) for j in range(half)], axis=1)
        both = jnp.dot(onehot, halves, preferred_element_type=f32)
        return jnp.where(high, both[:, TB:], both[:, :TB])

    for k in range(pair_rows):
        index = _column(rows_ref[k:k + 1].astype(f32)).astype(jnp.int32)
        order_ref[pl.ds(k, TB, stride=pair_rows), :] = pick(index, TB)
    early_ref[...] = order_ref[...].astype(bf16).reshape(bound_blocks * 8, 16, TB)
    out = [pltpu.make_async_copy(early_ref, send_hbm.at[:, 0:16, :], sems.at[9]),
           pltpu.make_async_copy(scaled_ref, scaled_hbm, sems.at[10])]
    for copy in out:
        copy.start()
    sub = lax.broadcasted_iota(jnp.int32, (16, TB), 0)
    index = jnp.zeros((16, TB), jnp.int32)
    for j in range(4):
        index = jnp.where(sub == j, hub_ref[j], index)
    hub = pick(index, 16)[:8]

    for copy in copies[4:]:
        copy.wait()
    for b in range(own_blocks):
        part = slice(b * TB, (b + 1) * TB)
        weighted_ref[part] = (_column(root[b:b + 1]) * cotangent_ref[part].astype(f32)).astype(bf16)
    live = live_ref[0]

    def step(t):
        products = []
        for k in range(GROUP):
            target = target_ref[t + k]
            w = weighted_ref[pl.ds(pl.multiple_of(target * TB, TB), TB), :]
            products.append(lax.dot_general(
                tiles_ref[t + k], w, (((0,), (0,)), ((), ())), preferred_element_type=f32))
        for k in range(GROUP):
            slots_ref[source_ref[t + k]] += jnp.where(t + k < live, products[k], 0.0)

    _tile_loop(live, step)
    out.append(pltpu.make_async_copy(slots_ref.at[0:own_blocks], local_hbm, sems.at[11]))
    out[-1].start()
    for i in range(bound_blocks):
        late_ref[8 * i:8 * i + 8, 0:16, :] = slots_ref[own_blocks + i].astype(bf16).reshape(8, 16, TB)
    first = lax.broadcasted_iota(jnp.int32, (16, 8, TB), 1) < 4
    hub_tile = jnp.broadcast_to(hub[None], (16, 8, TB))
    for h in range(slots_ref.shape[0] - own_blocks - bound_blocks):
        x = slots_ref[own_blocks + bound_blocks + h].reshape(16, 8, TB)
        odd = jnp.where(first, hub_tile, x)
        even = jnp.where(first, hub_tile, pltpu.roll(x, 4, 1))
        pair = jnp.stack([even, odd], axis=1).reshape(32, 8, TB)
        late_ref[32 * h:32 * h + 32, 16:24, :] = pair.astype(bf16)
    out.append(pltpu.make_async_copy(late_ref, send_hbm.at[:, 16:40, :], sems.at[12]))
    out[-1].start()
    for copy in out:
        copy.wait()


def _after_kernel(live_ref, target_ref, source_ref, hub_ref, degrees_ref, rows_ref, arrived_ref, local_ref,
                  scaled_ref, tiles_ref, out_ref, source_rows_ref, forward_ref, gradient_ref):
    f32, bf16 = jnp.float32, jnp.bfloat16
    own_blocks = degrees_ref.shape[0]
    bound_blocks = rows_ref.shape[0]
    for b in range(own_blocks):
        source_rows_ref[b] = scaled_ref[b * TB:(b + 1) * TB]
    for i in range(bound_blocks):
        source_rows_ref[own_blocks + i] = arrived_ref[8 * i:8 * i + 8, 0:16, :].reshape(TB, TB)
    first = lax.broadcasted_iota(jnp.int32, (16, 8, TB), 1) < 4
    hub_total = jnp.zeros((8, TB), f32)
    for h in range(source_rows_ref.shape[0] - own_blocks - bound_blocks):
        x = arrived_ref[32 * h:32 * h + 32, 32:40, :].astype(f32)
        hub_total = hub_total + jnp.sum(x, axis=0)
        x = x.reshape(16, 2, 8, TB)
        merged = jnp.where(first, x[:, 0], pltpu.roll(x[:, 1], 4, 1))
        source_rows_ref[own_blocks + bound_blocks + h] = merged.reshape(TB, TB).astype(bf16)

    forward_ref[...] = jnp.zeros(forward_ref.shape, f32)
    live = live_ref[0]

    def step(t):
        products = [
            jnp.dot(tiles_ref[t + k], source_rows_ref[source_ref[t + k]], preferred_element_type=f32)
            for k in range(GROUP)
        ]
        for k in range(GROUP):
            forward_ref[target_ref[t + k]] += jnp.where(t + k < live, products[k], 0.0)

    _tile_loop(live, step)

    returned = arrived_ref[:, 16:32, :].reshape(bound_blocks * TB, TB)
    sub = lax.broadcasted_iota(jnp.int32, (TB, TB), 0)
    for b in range(own_blocks):
        onehot = jnp.concatenate(
            [(jnp.broadcast_to(rows_ref[i:i + 1], (TB, TB)) == sub + b * TB).astype(f32).astype(bf16)
             for i in range(bound_blocks)], axis=1)
        part = slice(b * TB, (b + 1) * TB)
        gradient_ref[part] = local_ref[b] + jnp.dot(onehot, returned, preferred_element_type=f32)
    for j in range(4):
        row = pl.ds(hub_ref[j], 1)
        gradient_ref[row, :] = gradient_ref[row, :] + hub_total[4 + j:5 + j]

    root = lax.rsqrt(degrees_ref[...].astype(f32))
    replicas = out_ref.shape[0]
    each = own_blocks // replicas
    for b in range(own_blocks):
        column = _column(root[b:b + 1])
        c, at = b // each, (b % each) * TB
        out_ref[c, at:at + TB] = (column * forward_ref[b]).astype(bf16)
        at += each * TB
        out_ref[c, at:at + TB] = (column * gradient_ref[b * TB:(b + 1) * TB]).astype(bf16)


def body(embedding, cotangent, degrees, tile_values, tile_target, tile_source, live_tile_count, send_rows, hub_rows):
    f32, bf16 = jnp.float32, jnp.bfloat16
    own_rows, width = embedding.shape
    slots = tile_values.shape[2]
    partitions, pair_rows = send_rows.shape[1:]
    hubs = hub_rows.shape[1]
    replicas = lax.axis_size("rep")
    own_blocks = own_rows // TB
    source_blocks = (own_rows + partitions * (pair_rows + hubs)) // TB
    tiles = tile_values.reshape(slots, TB, TB)
    small = (live_tile_count.reshape(1), tile_target.reshape(slots), tile_source.reshape(slots), hub_rows.reshape(hubs))
    degree_blocks = degrees.reshape(own_blocks, TB)
    rows = send_rows.reshape(partitions * pair_rows // TB, TB)
    rows_by_place = send_rows[0].T
    in_smem = pl.BlockSpec(memory_space=pltpu.SMEM)
    in_hbm = pl.BlockSpec(memory_space=pltpu.HBM)
    in_vmem = pl.BlockSpec(memory_space=pltpu.VMEM)
    shape = jax.ShapeDtypeStruct
    pair = 2 * (pair_rows + hubs)

    def held(space, array):
        return space(array.shape, array.dtype)

    send, local, scaled = pl.pallas_call(
        _before_kernel,
        out_shape=(
            shape((partitions, pair, width), bf16), shape((own_blocks, TB, width), f32),
            shape((own_rows, width), bf16)),
        in_specs=[in_hbm] * 9,
        out_specs=(in_hbm,) * 3,
        scratch_shapes=[held(pltpu.SMEM, x) for x in small] + [
            held(pltpu.VMEM, x) for x in (degree_blocks, rows_by_place, embedding, cotangent, tiles)] + [
            pltpu.VMEM((partitions, pair_rows, width), bf16),
            pltpu.VMEM((partitions, pair - pair_rows, width), bf16),
            pltpu.VMEM((own_rows, width), bf16),
            pltpu.VMEM((own_rows, width), bf16),
            pltpu.VMEM((source_blocks, TB, width), f32),
            pltpu.VMEM((partitions * pair_rows, width), f32),
            pltpu.SemaphoreType.DMA((13,)),
        ],
        name="before",
    )(*small, degree_blocks, rows_by_place, embedding, cotangent, tiles)

    arrived = lax.all_to_all(send, "dom", split_axis=0, concat_axis=0, tiled=True)

    exchange = pl.pallas_call(
        _after_kernel,
        out_shape=shape((replicas, 2 * own_rows // replicas, width), bf16),
        in_specs=[in_smem] * 4 + [in_vmem] * 6,
        out_specs=in_vmem,
        scratch_shapes=[
            pltpu.VMEM((source_blocks, TB, width), bf16),
            pltpu.VMEM((own_blocks, TB, width), f32),
            pltpu.VMEM((own_rows, width), f32),
        ],
        compiler_params=pltpu.CompilerParams(vmem_limit_bytes=20 << 20),
        name="after",
    )(*small, degree_blocks, rows, arrived, local, scaled, tiles)

    parts = lax.all_to_all(exchange, "rep", split_axis=0, concat_axis=0, tiled=True)
    total = jnp.sum(parts.astype(f32), axis=0).astype(bf16)
    out_rows = own_rows // replicas
    return total[:out_rows], total[out_rows:]


def solution(mesh):
    placed = (
        P("dom", None),
        P("dom", None),
        P("dom"),
        P("dom", "rep", None, None, None),
        P("dom", "rep", None),
        P("dom", "rep", None),
        P("dom", "rep"),
        P("dom", None, None),
        P("dom", None),
    )
    return jax.shard_map(
        body,
        mesh=mesh,
        in_specs=placed,
        out_specs=(P(("dom", "rep"), None), P(("dom", "rep"), None)),
        check_vma=False,
    )
```

```python
import jax
import jax.numpy as jnp
from jax import lax
from jax.experimental import pallas as pl
from jax.experimental.pallas import tpu as pltpu
from jax.sharding import PartitionSpec as P

TB = 128
GROUP = 16


def _column(row):
    return jnp.broadcast_to(row, (TB, TB)).T


def _tile_loop(live, step):
    def group(g, carry):
        step(g * GROUP)
        return carry

    lax.fori_loop(0, (live + GROUP - 1) // GROUP, group, 0)


def _fetch(pairs, sems):
    copies = [pltpu.make_async_copy(src, dst, sems.at[i]) for i, (src, dst) in enumerate(pairs)]
    for copy in copies:
        copy.start()
    return copies


def _before_kernel(live_hbm, target_hbm, source_hbm, hub_hbm, degrees_hbm, rows_hbm, embedding_hbm, cotangent_hbm,
                   tiles_hbm, send_hbm, local_hbm, scaled_hbm, live_ref, target_ref, source_ref, hub_ref, degrees_ref,
                   rows_ref, embedding_ref, cotangent_ref, tiles_ref, early_ref, late_ref, scaled_ref, weighted_ref,
                   slots_ref, order_ref, sems):
    f32, bf16 = jnp.float32, jnp.bfloat16
    copies = _fetch((
        (degrees_hbm, degrees_ref), (embedding_hbm, embedding_ref), (rows_hbm, rows_ref), (hub_hbm, hub_ref),
        (cotangent_hbm, cotangent_ref), (live_hbm, live_ref), (target_hbm, target_ref), (source_hbm, source_ref),
        (tiles_hbm, tiles_ref)), sems)
    own_blocks = degrees_ref.shape[0]
    half = own_blocks // 2
    pair_rows = rows_ref.shape[0]
    bound_blocks = send_hbm.shape[0] // 8
    slots_ref[...] = jnp.zeros(slots_ref.shape, f32)
    for copy in copies[:4]:
        copy.wait()
    root = lax.rsqrt(degrees_ref[...].astype(f32))
    for b in range(own_blocks):
        part = slice(b * TB, (b + 1) * TB)
        scaled_ref[part] = (_column(root[b:b + 1]) * embedding_ref[part].astype(f32)).astype(bf16)

    halves = jnp.concatenate([scaled_ref[:half * TB], scaled_ref[half * TB:]], axis=1)
    lane = lax.broadcasted_iota(jnp.int32, (TB, TB), 1)

    def pick(index, count):
        high = index >= half * TB
        low = jnp.where(high, index - half * TB, index)
        onehot = jnp.concatenate(
            [(low == lane[:count] + j * TB).astype(f32).astype(bf16) for j in range(half)], axis=1)
        both = jnp.dot(onehot, halves, preferred_element_type=f32)
        return jnp.where(high, both[:, TB:], both[:, :TB])

    for k in range(pair_rows):
        index = _column(rows_ref[k:k + 1].astype(f32)).astype(jnp.int32)
        order_ref[pl.ds(k, TB, stride=pair_rows), :] = pick(index, TB)
    early_ref[...] = order_ref[...].astype(bf16).reshape(bound_blocks * 8, 16, TB)
    out = [pltpu.make_async_copy(early_ref, send_hbm.at[:, 0:16, :], sems.at[9]),
           pltpu.make_async_copy(scaled_ref, scaled_hbm, sems.at[10])]
    for copy in out:
        copy.start()
    sub = lax.broadcasted_iota(jnp.int32, (16, TB), 0)
    index = jnp.zeros((16, TB), jnp.int32)
    for j in range(4):
        index = jnp.where(sub == j, hub_ref[j], index)
    hub = pick(index, 16)[:8]

    for copy in copies[4:]:
        copy.wait()
    for b in range(own_blocks):
        part = slice(b * TB, (b + 1) * TB)
        weighted_ref[part] = (_column(root[b:b + 1]) * cotangent_ref[part].astype(f32)).astype(bf16)
    live = live_ref[0]

    def step(t):
        products = []
        for k in range(GROUP):
            target = target_ref[t + k]
            w = weighted_ref[pl.ds(pl.multiple_of(target * TB, TB), TB), :]
            products.append(lax.dot_general(
                tiles_ref[t + k], w, (((0,), (0,)), ((), ())), preferred_element_type=f32))
        for k in range(GROUP):
            slots_ref[source_ref[t + k]] += jnp.where(t + k < live, products[k], 0.0)

    _tile_loop(live, step)
    out.append(pltpu.make_async_copy(slots_ref.at[0:own_blocks], local_hbm, sems.at[11]))
    out[-1].start()
    for i in range(bound_blocks):
        late_ref[8 * i:8 * i + 8, 0:16, :] = slots_ref[own_blocks + i].astype(bf16).reshape(8, 16, TB)
    first = lax.broadcasted_iota(jnp.int32, (16, 8, TB), 1) < 4
    hub_tile = jnp.broadcast_to(hub[None], (16, 8, TB))
    for h in range(slots_ref.shape[0] - own_blocks - bound_blocks):
        x = slots_ref[own_blocks + bound_blocks + h].reshape(16, 8, TB)
        odd = jnp.where(first, hub_tile, x)
        even = jnp.where(first, hub_tile, pltpu.roll(x, 4, 1))
        pair = jnp.stack([even, odd], axis=1).reshape(32, 8, TB)
        late_ref[32 * h:32 * h + 32, 16:24, :] = pair.astype(bf16)
    out.append(pltpu.make_async_copy(late_ref, send_hbm.at[:, 16:40, :], sems.at[12]))
    out[-1].start()
    for copy in out:
        copy.wait()


def _after_kernel(live_ref, target_ref, source_ref, hub_ref, degrees_ref, rows_ref, arrived_ref, local_ref,
                  scaled_ref, tiles_ref, out_ref, source_rows_ref, forward_ref, gradient_ref):
    f32, bf16 = jnp.float32, jnp.bfloat16
    own_blocks = degrees_ref.shape[0]
    bound_blocks = rows_ref.shape[0]
    for b in range(own_blocks):
        source_rows_ref[b] = scaled_ref[b * TB:(b + 1) * TB]
    for i in range(bound_blocks):
        source_rows_ref[own_blocks + i] = arrived_ref[8 * i:8 * i + 8, 0:16, :].reshape(TB, TB)
    first = lax.broadcasted_iota(jnp.int32, (16, 8, TB), 1) < 4
    hub_total = jnp.zeros((8, TB), f32)
    for h in range(source_rows_ref.shape[0] - own_blocks - bound_blocks):
        x = arrived_ref[32 * h:32 * h + 32, 32:40, :].astype(f32)
        hub_total = hub_total + jnp.sum(x, axis=0)
        x = x.reshape(16, 2, 8, TB)
        merged = jnp.where(first, x[:, 0], pltpu.roll(x[:, 1], 4, 1))
        source_rows_ref[own_blocks + bound_blocks + h] = merged.reshape(TB, TB).astype(bf16)

    forward_ref[...] = jnp.zeros(forward_ref.shape, f32)
    live = live_ref[0]

    def step(t):
        products = [
            jnp.dot(tiles_ref[t + k], source_rows_ref[source_ref[t + k]], preferred_element_type=f32)
            for k in range(GROUP)
        ]
        for k in range(GROUP):
            forward_ref[target_ref[t + k]] += jnp.where(t + k < live, products[k], 0.0)

    _tile_loop(live, step)

    returned = arrived_ref[:, 16:32, :].reshape(bound_blocks * TB, TB)
    sub = lax.broadcasted_iota(jnp.int32, (TB, TB), 0)
    for b in range(own_blocks):
        onehot = jnp.concatenate(
            [(jnp.broadcast_to(rows_ref[i:i + 1], (TB, TB)) == sub + b * TB).astype(f32).astype(bf16)
             for i in range(bound_blocks)], axis=1)
        part = slice(b * TB, (b + 1) * TB)
        gradient_ref[part] = local_ref[b] + jnp.dot(onehot, returned, preferred_element_type=f32)
    for j in range(4):
        row = pl.ds(hub_ref[j], 1)
        gradient_ref[row, :] = gradient_ref[row, :] + hub_total[4 + j:5 + j]

    root = lax.rsqrt(degrees_ref[...].astype(f32))
    replicas = out_ref.shape[0]
    each = own_blocks // replicas
    for b in range(own_blocks):
        column = _column(root[b:b + 1])
        c, at = b // each, (b % each) * TB
        out_ref[c, at:at + TB] = (column * forward_ref[b]).astype(bf16)
        at += each * TB
        out_ref[c, at:at + TB] = (column * gradient_ref[b * TB:(b + 1) * TB]).astype(bf16)


def body(embedding, cotangent, degrees, tile_values, tile_target, tile_source, live_tile_count, send_rows, hub_rows):
    f32, bf16 = jnp.float32, jnp.bfloat16
    own_rows, width = embedding.shape
    slots = tile_values.shape[2]
    partitions, pair_rows = send_rows.shape[1:]
    hubs = hub_rows.shape[1]
    replicas = lax.axis_size("rep")
    own_blocks = own_rows // TB
    source_blocks = (own_rows + partitions * (pair_rows + hubs)) // TB
    tiles = tile_values.reshape(slots, TB, TB)
    small = (live_tile_count.reshape(1), tile_target.reshape(slots), tile_source.reshape(slots), hub_rows.reshape(hubs))
    degree_blocks = degrees.reshape(own_blocks, TB)
    rows = send_rows.reshape(partitions * pair_rows // TB, TB)
    rows_by_place = send_rows[0].T
    in_smem = pl.BlockSpec(memory_space=pltpu.SMEM)
    in_hbm = pl.BlockSpec(memory_space=pltpu.HBM)
    in_vmem = pl.BlockSpec(memory_space=pltpu.VMEM)
    shape = jax.ShapeDtypeStruct
    pair = 2 * (pair_rows + hubs)

    def held(space, array):
        return space(array.shape, array.dtype)

    send, local, scaled = pl.pallas_call(
        _before_kernel,
        out_shape=(
            shape((partitions, pair, width), bf16), shape((own_blocks, TB, width), f32),
            shape((own_rows, width), bf16)),
        in_specs=[in_hbm] * 9,
        out_specs=(in_hbm,) * 3,
        scratch_shapes=[held(pltpu.SMEM, x) for x in small] + [
            held(pltpu.VMEM, x) for x in (degree_blocks, rows_by_place, embedding, cotangent, tiles)] + [
            pltpu.VMEM((partitions, pair_rows, width), bf16),
            pltpu.VMEM((partitions, pair - pair_rows, width), bf16),
            pltpu.VMEM((own_rows, width), bf16),
            pltpu.VMEM((own_rows, width), bf16),
            pltpu.VMEM((source_blocks, TB, width), f32),
            pltpu.VMEM((partitions * pair_rows, width), f32),
            pltpu.SemaphoreType.DMA((13,)),
        ],
        name="before",
    )(*small, degree_blocks, rows_by_place, embedding, cotangent, tiles)

    arrived = lax.all_to_all(send, "dom", split_axis=0, concat_axis=0, tiled=True)

    exchange = pl.pallas_call(
        _after_kernel,
        out_shape=shape((replicas, 2 * own_rows // replicas, width), bf16),
        in_specs=[in_smem] * 4 + [in_vmem] * 6,
        out_specs=in_vmem,
        scratch_shapes=[
            pltpu.VMEM((source_blocks, TB, width), bf16),
            pltpu.VMEM((own_blocks, TB, width), f32),
            pltpu.VMEM((own_rows, width), f32),
        ],
        compiler_params=pltpu.CompilerParams(vmem_limit_bytes=20 << 20),
        name="after",
    )(*small, degree_blocks, rows, arrived, local, scaled, tiles)

    parts = lax.all_to_all(exchange, "rep", split_axis=0, concat_axis=0, tiled=True)
    total = jnp.sum(parts.astype(f32), axis=0).astype(bf16)
    out_rows = own_rows // replicas
    return total[:out_rows], total[out_rows:]


def solution(mesh):
    placed = (
        P("dom", None),
        P("dom", None),
        P("dom"),
        P("dom", "rep", None, None, None),
        P("dom", "rep", None),
        P("dom", "rep", None),
        P("dom", "rep"),
        P("dom", None, None),
        P("dom", None),
    )
    return jax.shard_map(
        body,
        mesh=mesh,
        in_specs=placed,
        out_specs=(P(("dom", "rep"), None), P(("dom", "rep"), None)),
        check_vma=False,
    )
```
